32 devices in a mesh: img: 8 (over z, y), rep: 4 (over x, core).
Axes of the slice: x: 2, y: 2, z: 4, core: 2. Of those that a mesh axis runs over, the one named last changes fastest.
Arguments:
- descriptors: bfloat16 [16, 256, 1024], P('img', 'rep'), may hold values from -0.5 to 0.5
- cell_counts: int32 [16, 256], P('img', 'rep'), may hold values from 1 to 8
- pair_images: int32 [64, 2], P('img'), may hold values from 0 to 15, as said below
- query_cells: int32 [64, 16], P('img'), may hold values from 0 to 255
- cand_cells: int32 [64, 4, 16], P('img', 'rep'), may hold values from 0 to 255, as said below
- cand_counts: int32 [64, 4], P('img', 'rep'), may hold values from 8 to 16, as said below
Outputs:
- matches: float32 [64, 2, 128], P('img')
- image_score: float32 [16], P('img')
The draws below stay inside these ranges and needn't reach their ends.
Inputs may be any that keep to these rules, and one draw needn't show every extreme that they name: `pair_images`: the pairs are numbered by blocks of 8: pair k * 8 + j has its first image among images k * 2 to k * 2 + 1 and its second among images j * 2 to j * 2 + 1; the two images of a pair differ. cand_cells[p, r, s] lies in quarter r, between r * 64 and r * 64 + 63; cells may repeat. `cand_counts`: every count is 8 or 16, and every draw holds at least one count of 16.
All inputs are finite; a program needn't handle non-finite values.
Results may differ from the reference program's by a relative error of at most 0.0003.
Values may be sent and summed in bfloat16 or wider, within the bound.
A program may use at most 64 MiB of HBM per device.

```python
import jax
import jax.numpy as jnp
from jax import lax

DESC = 128
KP = 8
CELLS = 256
IMG_DEV = 2
QCELL = 16
SLOT = 16
QDESC = 128
IMAGES = 16
PAIRS = 64
N_IMG = 8
N_REP = 4


def draw_pair_images(key, part):
    index = jnp.arange(N_IMG * N_IMG, dtype=jnp.int32)
    owner = index // N_IMG
    partner = index % N_IMG
    key_first = jax.random.fold_in(key, 11)
    key_second = jax.random.fold_in(key, 12)
    key_same = jax.random.fold_in(key, 13)
    local_first = jax.random.randint(key_first, (N_IMG * N_IMG,), 0, IMG_DEV, dtype=jnp.int32)
    local_any = jax.random.randint(key_second, (N_IMG * N_IMG,), 0, IMG_DEV, dtype=jnp.int32)
    local_other = jax.random.randint(key_same, (N_IMG * N_IMG,), 0, IMG_DEV - 1, dtype=jnp.int32)
    local_other = jnp.where(local_other >= local_first, local_other + 1, local_other)
    local_second = jnp.where(owner == partner, local_other, local_any)
    first = owner * IMG_DEV + local_first
    second = partner * IMG_DEV + local_second
    return jnp.stack([first, second], axis=1).astype(jnp.int32)


def draw_cand_cells(key, part):
    share = CELLS // N_REP
    offsets = jax.random.randint(jax.random.fold_in(key, 21), (N_IMG * N_IMG, N_REP, SLOT), 0, share, dtype=jnp.int32)
    quarter = jnp.arange(N_REP, dtype=jnp.int32)[None, :, None] * share
    return (offsets + quarter).astype(jnp.int32)


def draw_cand_counts(key, part):
    divisor = jax.random.randint(jax.random.fold_in(key, 31), (N_IMG * N_IMG * N_REP,), 1, 3, dtype=jnp.int32)
    counts = SLOT // divisor
    spot = jax.random.randint(jax.random.fold_in(key, 32), (), 0, N_IMG * N_IMG * N_REP, dtype=jnp.int32)
    counts = jnp.where(jnp.arange(N_IMG * N_IMG * N_REP, dtype=jnp.int32) == spot, SLOT, counts)
    return counts.reshape(N_IMG * N_IMG, N_REP).astype(jnp.int32)


def touch_ends(array, own_key, smallest, largest):
    spot = [jax.random.randint(jax.random.fold_in(own_key, axis), (), 0, length) for axis, length in enumerate(array.shape)]
    longest = array.shape.index(max(array.shape))
    next_to = spot[:longest] + [(spot[longest] + 1) % array.shape[longest]] + spot[longest + 1:]
    return array.at[tuple(spot)].set(smallest).at[tuple(next_to)].set(largest)


def levels(own_key, dims, shards, low, largest):
    gain, own = 1.0, jax.random.fold_in(own_key, 6)
    for position, blocks in shards:
        heights = jnp.exp(jax.random.uniform(jax.random.fold_in(own, position), (blocks,), jnp.float32, low / len(shards), largest / len(shards)))
        gain = gain * jnp.repeat(heights, dims[position] // blocks).reshape([-1 if axis == position else 1 for axis in range(len(dims))])
    return gain


def gaussian(rng, shape, width, limit, split=(), kind=jnp.bfloat16):
    entries = width * jax.random.normal(rng, shape, jnp.float32)
    if split:
        entries = entries * levels(rng, shape, split, -0.22, 0.18)
    return jnp.clip(entries, -limit, limit).astype(kind)


def setup_inputs(seed: int = 0) -> dict:
    keys = jax.random.split(jax.random.key(seed), 7)
    descriptors = gaussian(keys[0], (IMAGES, CELLS, KP * DESC), 0.0884, 0.5, ((0, 8), (1, 4)))
    cell_counts = touch_ends(jax.random.randint(keys[1], (IMAGES, CELLS), 1, KP + 1), jax.random.fold_in(keys[1], 1), 1, KP).astype(jnp.int32)
    pair_images = draw_pair_images(jax.random.fold_in(keys[6], 71), 0)
    query_cells = touch_ends(jax.random.randint(keys[3], (PAIRS, QCELL), 0, CELLS), jax.random.fold_in(keys[3], 1), 0, CELLS - 1).astype(jnp.int32)
    cand_cells = draw_cand_cells(jax.random.fold_in(keys[6], 71), 0)
    cand_counts = draw_cand_counts(jax.random.fold_in(keys[6], 71), 0)
    return {"descriptors": descriptors, "cell_counts": cell_counts, "pair_images": pair_images, "query_cells": query_cells, "cand_cells": cand_cells, "cand_counts": cand_counts}


distant = 1.0e9


def reference(descriptors, cell_counts, pair_images, query_cells, cand_cells, cand_counts):
    flat = descriptors.reshape(IMAGES * CELLS, KP * DESC)
    flat_counts = cell_counts.reshape(IMAGES * CELLS)
    first = pair_images[:, 0].astype(jnp.int32)
    second = pair_images[:, 1].astype(jnp.int32)
    query_rows = (first[:, None] * CELLS + query_cells).astype(jnp.int32)
    cand_rows = (second[:, None, None] * CELLS + cand_cells).astype(jnp.int32)
    slot_ids = jnp.arange(KP, dtype=jnp.int32)
    cand_ids = jnp.arange(SLOT, dtype=jnp.int32)

    def one_pair(index):
        qrow = query_rows[index]
        crow = cand_rows[index].reshape(N_REP * SLOT)
        queries = flat[qrow].reshape(QDESC, DESC).astype(jnp.float32)
        qlive = (slot_ids[None, :] < flat_counts[qrow][:, None]).reshape(QDESC)
        cands = flat[crow].reshape(N_REP * SLOT * KP, DESC).astype(jnp.float32)
        cell_live = cand_ids[None, :] < cand_counts[index][:, None]
        slot_live = slot_ids[None, None, :] < flat_counts[crow].reshape(N_REP, SLOT)[:, :, None]
        clive = (cell_live[:, :, None] & slot_live).reshape(N_REP * SLOT * KP)
        qnorm = jnp.sum(queries * queries, axis=1)
        cnorm = jnp.sum(cands * cands, axis=1)
        inner = jnp.dot(queries, cands.T, precision=lax.Precision.HIGHEST, preferred_element_type=jnp.float32)
        dist = qnorm[:, None] + cnorm[None, :] - 2.0 * inner
        dist = jnp.where(clive[None, :], dist, jnp.float32(distant))
        lowest = -lax.top_k(-dist, 2)[0]
        best = jnp.where(qlive, lowest[:, 0], jnp.float32(0.0))
        runner = jnp.where(qlive, lowest[:, 1], jnp.float32(0.0))
        margin = jnp.where(qlive, (runner - best) / (runner + 1.0), jnp.float32(0.0))
        score = jnp.sum(margin) / jnp.sum(qlive.astype(jnp.float32))
        return jnp.stack([best, runner]), score

    matches, scores = lax.map(one_pair, jnp.arange(PAIRS, dtype=jnp.int32))
    image_score = jnp.zeros((IMAGES,), jnp.float32).at[first].add(scores).at[second].add(scores)
    return matches, image_score
```

```python
import functools

import jax
import jax.numpy as jnp
from jax import lax
from jax.experimental import pallas as pl
from jax.experimental.pallas import tpu as pltpu
from jax.sharding import PartitionSpec as P

DESC = 128
MESH = pl.DeviceIdType.MESH
distant = 1.0e9
far_entry = 32768.0
dead_mark = -1.0e9
f32, bf16, i32 = jnp.float32, jnp.bfloat16, jnp.int32


def partner(me, step, size):
    other, bit = 0, 1
    while bit < size:
        other = other + ((me // bit + step // bit) % 2) * bit
        bit *= 2
    return other


def repeat(first, last, body):
    if last - first <= 8:
        for t in range(first, last):
            body(t)
    else:
        lax.fori_loop(first, last, lambda t, c: (body(t), c)[1], 0)


def dot_t(a, b):
    return lax.dot_general(a, b, (((1,), (1,)), ((), ())), preferred_element_type=f32)


def split(square):
    high = square.astype(bf16)
    return high, (square - high.astype(f32)).astype(bf16)


def column(row, length):
    rows = lax.broadcasted_iota(i32, (length, length), 0)
    cols = lax.broadcasted_iota(i32, (length, length), 1)
    return jnp.sum(jnp.where(rows == cols, row, 0.0), axis=1, keepdims=True)


def merge(a, b):
    low = jnp.minimum(a[0], b[0])
    high = jnp.minimum(jnp.maximum(a[0], b[0]), jnp.minimum(a[1], b[1]))
    return low, high


def lowest_two(d):
    half = d.shape[0] // 2
    a, b = d[:half], d[half:]
    two = (jnp.minimum(a, b), jnp.maximum(a, b))
    while half > 1:
        half //= 2
        two = merge((two[0][:half], two[1][:half]), (two[0][half:], two[1][half:]))
    return two


def kernel(
    n, m,
    desc, counts, pairs, qcells, ccells, ccounts,
    matches, scores,
    whole, lists_out, lists_in, cands_out, cands_in, rhs, qnorm, part_out, own, arr,
    ag_send, ag_recv, fw_send, fw_recv, list_send, list_recv, cand_send, cand_recv,
    own_send, own_recv, arr_send, arr_recv,
):
    me, r = lax.axis_index("img"), lax.axis_index("rep")
    img_dev, share, width = desc.shape
    rows = img_dev * share
    kp = width // DESC
    slots = ccells.shape[2]
    qn = qcells.shape[1]
    mate, across = partner(r, 1, m), partner(r, 2, m)

    def remote(src, dst, send, recv, img, rep):
        return pltpu.make_async_remote_copy(
            src_ref=src, dst_ref=dst, send_sem=send, recv_sem=recv,
            device_id=(img, rep), device_id_type=MESH,
        )

    barrier = pltpu.get_barrier_semaphore()

    def greet_all(t):
        other = (me * m + r + t) % (n * m)
        pl.semaphore_signal(barrier, inc=1, device_id=(other // m, other % m), device_id_type=MESH)

    lax.fori_loop(1, n * m, lambda t, c: (greet_all(t), c)[1], 0)

    slot_of = lax.broadcasted_iota(i32, (share, width), 1) // DESC
    for i in range(img_dev):
        live = column(counts[i : i + 1, :].astype(f32), share)
        marked = jnp.where(slot_of.astype(f32) < live, desc[i].astype(f32), far_entry)
        whole[r, i * share : (i + 1) * share, :] = marked.astype(bf16)

    second = pairs[:, 1:2] % img_dev
    wanted = second * share + ccells[:, 0, :] % share
    wanted = jnp.where(lax.broadcasted_iota(i32, (n, slots), 1) < ccounts[...], wanted, -1)
    wanted = wanted.astype(f32)
    for j in range(n):
        spread = jnp.broadcast_to(column(wanted[j : j + 1, :], slots), (slots, rows))
        lists_out[j] = spread.astype(i32)
    lists_in[me] = lists_out[me]

    pl.semaphore_wait(barrier, n * m - 1)

    def send_list(t):
        k = partner(me, t, n)
        remote(lists_out.at[k], lists_in.at[me], list_send, list_recv.at[me], k, r).start()

    repeat(1, n, send_list)

    def shard(owner, i):
        return whole.at[owner, pl.ds(i * share, share)]

    for i in range(img_dev):
        remote(shard(r, i), shard(r, i), ag_send, ag_recv.at[0, i], me, across).start()
    for i in range(img_dev):
        remote(shard(r, i), shard(r, i), ag_send, ag_recv.at[1, i], me, mate).start()

    group = n // 2
    lane = lax.broadcasted_iota(i32, (slots, rows), 1)
    for g in range(0, n, group):
        picks = []
        for t in range(g, g + group):
            k = partner(me, t, n)
            if t > 0:
                pltpu.make_async_copy(lists_out.at[k], lists_in.at[k], list_recv.at[k]).wait()
            picks.append(lists_in[k])
        asked = jnp.concatenate(picks, axis=0)
        lanes = lax.broadcasted_iota(i32, asked.shape, 1)
        chosen = (asked == lanes).astype(f32).astype(bf16)
        block = jnp.dot(chosen, whole[r], preferred_element_type=f32)
        block = jnp.where(asked[:, :1] < 0, far_entry, block).astype(bf16)
        for t in range(g, g + group):
            k = partner(me, t, n)
            part = block[(t - g) * slots : (t - g + 1) * slots]
            if t == 0:
                cands_in[me] = part
            else:
                cands_out[k] = part
        for t in range(max(g, 1), g + group):
            k = partner(me, t, n)
            remote(cands_out.at[k], cands_in.at[me], cand_send, cand_recv.at[me], k, r).start()

    for i in range(img_dev):
        pltpu.make_async_copy(shard(across, i), shard(across, i), ag_recv.at[0, i]).wait()
        remote(shard(across, i), shard(across, i), fw_send, fw_recv.at[i], me, mate).start()
    diagonal = partner(r, 3, m)
    for i in range(img_dev):
        pltpu.make_async_copy(shard(mate, i), shard(mate, i), ag_recv.at[1, i]).wait()
    for i in range(img_dev):
        pltpu.make_async_copy(shard(diagonal, i), shard(diagonal, i), fw_recv.at[i]).wait()

    first = pairs[:, 0:1] % img_dev
    cells = qcells[...]
    where = (cells // share) * rows + first * share + cells % share
    where = where.astype(f32)
    all_rows = m * rows
    picks = [
        jnp.broadcast_to(column(where[j : j + 1, :], qn), (qn, all_rows)) for j in range(n)
    ]
    asked = jnp.concatenate(picks, axis=0).astype(i32)
    chosen = (asked == lax.broadcasted_iota(i32, asked.shape, 1)).astype(f32).astype(bf16)
    found = jnp.dot(chosen, whole[...].reshape(all_rows, width), preferred_element_type=f32)
    found = found.astype(bf16)
    qd = qn * kp
    to = lax.broadcasted_iota(i32, (qd, qd), 0)
    at = lax.broadcasted_iota(i32, (qd, qd), 1)
    order = (at == (to % kp) * qn + to // kp).astype(f32).astype(bf16)
    ones = jnp.ones((qd, DESC), bf16)
    for j in range(n):
        mine = found[j * qn : (j + 1) * qn]
        stack = jnp.concatenate([mine[:, s * DESC : (s + 1) * DESC] for s in range(kp)], axis=0)
        query = jnp.dot(order, stack, preferred_element_type=f32)
        high, low = split(query * query)
        qnorm[j] = dot_t(jnp.ones((8, 2 * DESC), bf16), jnp.concatenate([high, low], axis=1))
        rhs[j] = jnp.concatenate([ones, ones, query.astype(bf16)], axis=1)

    def one_pair(t):
        j = partner(me, t, n)
        if not (isinstance(t, int) and t == 0):
            pltpu.make_async_copy(cands_out.at[j], cands_in.at[j], cand_recv.at[j]).wait()
        mine = cands_in[j]
        stack = jnp.concatenate([mine[:, s * DESC : (s + 1) * DESC] for s in range(kp)], axis=0)
        wide = stack.astype(f32)
        high, low = split(wide * wide)
        lhs = jnp.concatenate([high, low, (-2.0 * wide).astype(bf16)], axis=1)
        norm = qnorm[j][0:1]
        dist = jnp.minimum(dot_t(lhs, rhs[j]) + norm, distant)
        best, runner = lowest_two(dist)
        live = norm < distant
        two = jnp.concatenate(
            [jnp.where(live, best, dead_mark), jnp.where(live, runner, dead_mark)], axis=0
        )
        part_out[j] = two
        own[r, j] = two
        for d in range(1, m):
            to_rep = partner(r, d, m)
            remote(part_out.at[j], own.at[r, j], own_send, own_recv.at[r], me, to_rep).start()
        if not (isinstance(t, int) and t == 0):
            for d in range(m):
                to_rep = partner(r, d, m)
                remote(part_out.at[j], arr.at[r, me], arr_send, arr_recv.at[r], j, to_rep).start()

    one_pair(0)
    repeat(1, n, one_pair)

    for d in range(1, m):
        o = partner(r, d, m)
        pltpu.make_async_copy(own.at[o], own.at[o], own_recv.at[o]).wait()

    def gathered(buf):
        two = (buf[0, :, 0, :], buf[0, :, 1, :])
        for o in range(1, m):
            two = merge(two, (buf[o, :, 0, :], buf[o, :, 1, :]))
        return two

    def score_of(two):
        live = two[0] > 0.5 * dead_mark
        best, runner = jnp.where(live, two[0], 0.0), jnp.where(live, two[1], 0.0)
        margin = jnp.where(live, (runner - best) / (runner + 1.0), 0.0)
        total = jnp.sum(margin, axis=1, keepdims=True)
        return best, runner, total / jnp.sum(live.astype(f32), axis=1, keepdims=True)

    best, runner, score = score_of(gathered(own))
    matches[:, 0, :] = best
    matches[:, 1, :] = runner

    for o in range(m):
        arr[o, me] = own[o, me]
    for o in range(m):
        rest = arr.at[o, pl.ds(0, n - 1)]
        pltpu.make_async_copy(rest, rest, arr_recv.at[o]).wait()
    _, _, other_score = score_of(gathered(arr))
    asked_image = lists_in[:, 0, :][:, 0:1] // share
    for i in range(img_dev):
        scores[i] = jnp.sum(jnp.where(first == i, score, 0.0)) + jnp.sum(
            jnp.where(asked_image == i, other_score, 0.0)
        )

    def drain(ref, sem):
        pltpu.make_async_copy(ref, ref, sem).wait()

    drain(whole.at[pl.ds(0, 2)], ag_send)
    drain(whole.at[0], fw_send)
    drain(lists_out.at[pl.ds(0, n - 1)], list_send)
    drain(cands_out.at[pl.ds(0, n - 1)], cand_send)
    drain(own.at[pl.ds(0, m - 1)], own_send)
    drain(arr.at[:, pl.ds(0, n - 1)], arr_send)


def on_device(n, m, descriptors, cell_counts, pair_images, query_cells, cand_cells, cand_counts):
    img_dev, share, width = descriptors.shape
    rows, slots, qd = img_dev * share, cand_cells.shape[2], query_cells.shape[1] * width // DESC
    vmem = pl.BlockSpec(memory_space=pltpu.VMEM)
    dma = pltpu.SemaphoreType.DMA
    return pl.pallas_call(
        functools.partial(kernel, n, m),
        out_shape=(
            jax.ShapeDtypeStruct((n, 2, qd), f32),
            jax.ShapeDtypeStruct((img_dev,), f32),
        ),
        in_specs=[vmem] * 6,
        out_specs=(vmem, pl.BlockSpec(memory_space=pltpu.SMEM)),
        scratch_shapes=[
            pltpu.VMEM((m, rows, width), bf16),
            pltpu.VMEM((n, slots, rows), i32),
            pltpu.VMEM((n, slots, rows), i32),
            pltpu.VMEM((n, slots, width), bf16),
            pltpu.VMEM((n, slots, width), bf16),
            pltpu.VMEM((n, qd, 3 * DESC), bf16),
            pltpu.VMEM((n, 8, qd), f32),
            pltpu.VMEM((n, 2, qd), f32),
            pltpu.VMEM((m, n, 2, qd), f32),
            pltpu.VMEM((m, n, 2, qd), f32),
            dma, dma((2, img_dev)), dma, dma((img_dev,)),
            dma, dma((n,)), dma, dma((n,)),
            dma, dma((m,)), dma, dma((m,)),
        ],
        compiler_params=pltpu.CompilerParams(collective_id=0, has_side_effects=True),
    )(descriptors, cell_counts, pair_images, query_cells, cand_cells, cand_counts)


def solution(mesh):
    n, m = mesh.shape["img"], mesh.shape["rep"]
    in_specs = (
        P("img", "rep", None),
        P("img", "rep"),
        P("img", None),
        P("img", None),
        P("img", "rep", None),
        P("img", "rep"),
    )
    out_specs = (P("img", None, None), P("img"))
    return jax.shard_map(
        functools.partial(on_device, n, m),
        mesh=mesh, in_specs=in_specs, out_specs=out_specs, check_vma=False,
    )
```

```python
import functools

import jax
import jax.numpy as jnp
from jax import lax
from jax.experimental import pallas as pl
from jax.experimental.pallas import tpu as pltpu
from jax.sharding import PartitionSpec as P

DESC = 128
MESH = pl.DeviceIdType.MESH
distant = 1.0e9
far_entry = 32768.0
dead_mark = -1.0e9
f32, bf16, i32 = jnp.float32, jnp.bfloat16, jnp.int32


def partner(me, step, size):
    other, bit = 0, 1
    while bit < size:
        other = other + ((me // bit + step // bit) % 2) * bit
        bit *= 2
    return other


def repeat(first, last, body):
    if last - first <= 8:
        for t in range(first, last):
            body(t)
    else:
        lax.fori_loop(first, last, lambda t, c: (body(t), c)[1], 0)


def dot_t(a, b):
    return lax.dot_general(a, b, (((1,), (1,)), ((), ())), preferred_element_type=f32)


def split(square):
    high = square.astype(bf16)
    return high, (square - high.astype(f32)).astype(bf16)


def column(row, length):
    rows = lax.broadcasted_iota(i32, (length, length), 0)
    cols = lax.broadcasted_iota(i32, (length, length), 1)
    return jnp.sum(jnp.where(rows == cols, row, 0.0), axis=1, keepdims=True)


def merge(a, b):
    low = jnp.minimum(a[0], b[0])
    high = jnp.minimum(jnp.maximum(a[0], b[0]), jnp.minimum(a[1], b[1]))
    return low, high


def lowest_two(d):
    half = d.shape[0] // 2
    a, b = d[:half], d[half:]
    two = (jnp.minimum(a, b), jnp.maximum(a, b))
    while half > 1:
        half //= 2
        two = merge((two[0][:half], two[1][:half]), (two[0][half:], two[1][half:]))
    return two


def kernel(
    n, m,
    desc_hbm, counts_hbm, pairs_hbm, qcells_hbm, ccells_hbm, ccounts_hbm,
    matches, scores,
    desc, counts, pairs, qcells, ccells, ccounts, in_sem,
    whole, lists_out, lists_in, cands_out, cands_in, rhs, qnorm, part_out, own, arr,
    ag_send, ag_recv, fw_send, fw_recv, list_send, list_recv, cand_send, cand_recv,
    own_send, own_recv, arr_send, arr_recv,
):
    me, r = lax.axis_index("img"), lax.axis_index("rep")
    img_dev, share, width = desc.shape
    rows = img_dev * share
    kp = width // DESC
    slots = ccells.shape[2]
    qn = qcells.shape[1]
    mate, across = partner(r, 1, m), partner(r, 2, m)

    def remote(src, dst, send, recv, img, rep):
        return pltpu.make_async_remote_copy(
            src_ref=src, dst_ref=dst, send_sem=send, recv_sem=recv,
            device_id=(img, rep), device_id_type=MESH,
        )

    barrier = pltpu.get_barrier_semaphore()

    def greet_all(t):
        other = (me * m + r + t) % (n * m)
        pl.semaphore_signal(barrier, inc=1, device_id=(other // m, other % m), device_id_type=MESH)

    lax.fori_loop(1, n * m, lambda t, c: (greet_all(t), c)[1], 0)

    loads = [
        pltpu.make_async_copy(src, dst, in_sem.at[i])
        for i, (src, dst) in enumerate((
            (counts_hbm, counts), (desc_hbm, desc), (pairs_hbm, pairs),
            (ccells_hbm, ccells), (ccounts_hbm, ccounts), (qcells_hbm, qcells),
        ))
    ]
    for load in loads:
        load.start()
    for load in loads:
        load.wait()

    slot_of = lax.broadcasted_iota(i32, (share, width), 1) // DESC
    for i in range(img_dev):
        live = column(counts[i : i + 1, :].astype(f32), share)
        marked = jnp.where(slot_of.astype(f32) < live, desc[i].astype(f32), far_entry)
        whole[r, i * share : (i + 1) * share, :] = marked.astype(bf16)

    local = (pairs[...] % img_dev).astype(f32)
    first = column(local[0:1], n).astype(i32)
    second = column(local[1:2], n).astype(i32)
    live_cells = column(ccounts[...].astype(f32), n).astype(i32)
    wanted = second * share + ccells[:, 0, :] % share
    wanted = jnp.where(lax.broadcasted_iota(i32, (n, slots), 1) < live_cells, wanted, -1)
    wanted = wanted.astype(f32)
    for j in range(n):
        spread = jnp.broadcast_to(column(wanted[j : j + 1, :], slots), (slots, rows))
        lists_out[j] = spread.astype(i32)
    lists_in[me] = lists_out[me]

    pl.semaphore_wait(barrier, n * m - 1)

    def send_list(t):
        k = partner(me, t, n)
        remote(lists_out.at[k], lists_in.at[me], list_send, list_recv.at[me], k, r).start()

    repeat(1, n, send_list)

    def shard(owner, i):
        return whole.at[owner, pl.ds(i * share, share)]

    for i in range(img_dev):
        remote(shard(r, i), shard(r, i), ag_send, ag_recv.at[0, i], me, across).start()
    for i in range(img_dev):
        remote(shard(r, i), shard(r, i), ag_send, ag_recv.at[1, i], me, mate).start()

    group = n // 2
    lane = lax.broadcasted_iota(i32, (slots, rows), 1)
    for g in range(0, n, group):
        picks = []
        for t in range(g, g + group):
            k = partner(me, t, n)
            if t > 0:
                pltpu.make_async_copy(lists_out.at[k], lists_in.at[k], list_recv.at[k]).wait()
            picks.append(lists_in[k])
        asked = jnp.concatenate(picks, axis=0)
        lanes = lax.broadcasted_iota(i32, asked.shape, 1)
        chosen = (asked == lanes).astype(f32).astype(bf16)
        block = jnp.dot(chosen, whole[r], preferred_element_type=f32)
        block = jnp.where(asked[:, :1] < 0, far_entry, block).astype(bf16)
        for t in range(g, g + group):
            k = partner(me, t, n)
            part = block[(t - g) * slots : (t - g + 1) * slots]
            if t == 0:
                cands_in[me] = part
            else:
                cands_out[k] = part
        for t in range(max(g, 1), g + group):
            k = partner(me, t, n)
            remote(cands_out.at[k], cands_in.at[me], cand_send, cand_recv.at[me], k, r).start()

    for i in range(img_dev):
        pltpu.make_async_copy(shard(across, i), shard(across, i), ag_recv.at[0, i]).wait()
        remote(shard(across, i), shard(across, i), fw_send, fw_recv.at[i], me, mate).start()
    diagonal = partner(r, 3, m)
    for i in range(img_dev):
        pltpu.make_async_copy(shard(mate, i), shard(mate, i), ag_recv.at[1, i]).wait()
    for i in range(img_dev):
        pltpu.make_async_copy(shard(diagonal, i), shard(diagonal, i), fw_recv.at[i]).wait()

    cells = qcells[...]
    where = (cells // share) * rows + first * share + cells % share
    where = where.astype(f32)
    all_rows = m * rows
    picks = [
        jnp.broadcast_to(column(where[j : j + 1, :], qn), (qn, all_rows)) for j in range(n)
    ]
    asked = jnp.concatenate(picks, axis=0).astype(i32)
    chosen = (asked == lax.broadcasted_iota(i32, asked.shape, 1)).astype(f32).astype(bf16)
    found = jnp.dot(chosen, whole[...].reshape(all_rows, width), preferred_element_type=f32)
    found = found.astype(bf16)
    qd = qn * kp
    to = lax.broadcasted_iota(i32, (qd, qd), 0)
    at = lax.broadcasted_iota(i32, (qd, qd), 1)
    order = (at == (to % kp) * qn + to // kp).astype(f32).astype(bf16)
    ones = jnp.ones((qd, DESC), bf16)
    for j in range(n):
        mine = found[j * qn : (j + 1) * qn]
        stack = jnp.concatenate([mine[:, s * DESC : (s + 1) * DESC] for s in range(kp)], axis=0)
        query = jnp.dot(order, stack, preferred_element_type=f32)
        high, low = split(query * query)
        qnorm[j] = dot_t(jnp.ones((8, 2 * DESC), bf16), jnp.concatenate([high, low], axis=1))
        rhs[j] = jnp.concatenate([ones, ones, query.astype(bf16)], axis=1)

    def one_pair(t):
        j = partner(me, t, n)
        if not (isinstance(t, int) and t == 0):
            pltpu.make_async_copy(cands_out.at[j], cands_in.at[j], cand_recv.at[j]).wait()
        mine = cands_in[j]
        stack = jnp.concatenate([mine[:, s * DESC : (s + 1) * DESC] for s in range(kp)], axis=0)
        wide = stack.astype(f32)
        high, low = split(wide * wide)
        lhs = jnp.concatenate([high, low, (-2.0 * wide).astype(bf16)], axis=1)
        norm = qnorm[j][0:1]
        dist = jnp.minimum(dot_t(lhs, rhs[j]) + norm, distant)
        best, runner = lowest_two(dist)
        live = norm < distant
        two = jnp.concatenate(
            [jnp.where(live, best, dead_mark), jnp.where(live, runner, dead_mark)], axis=0
        )
        part_out[j] = two
        own[r, j] = two
        for d in range(1, m):
            to_rep = partner(r, d, m)
            remote(part_out.at[j], own.at[r, j], own_send, own_recv.at[r], me, to_rep).start()
        if not (isinstance(t, int) and t == 0):
            for d in range(m):
                to_rep = partner(r, d, m)
                remote(part_out.at[j], arr.at[r, me], arr_send, arr_recv.at[r], j, to_rep).start()

    one_pair(0)
    repeat(1, n, one_pair)

    for d in range(1, m):
        o = partner(r, d, m)
        pltpu.make_async_copy(own.at[o], own.at[o], own_recv.at[o]).wait()

    def gathered(buf):
        two = (buf[0, :, 0, :], buf[0, :, 1, :])
        for o in range(1, m):
            two = merge(two, (buf[o, :, 0, :], buf[o, :, 1, :]))
        return two

    def score_of(two):
        live = two[0] > 0.5 * dead_mark
        best, runner = jnp.where(live, two[0], 0.0), jnp.where(live, two[1], 0.0)
        margin = jnp.where(live, (runner - best) / (runner + 1.0), 0.0)
        total = jnp.sum(margin, axis=1, keepdims=True)
        return best, runner, total / jnp.sum(live.astype(f32), axis=1, keepdims=True)

    best, runner, score = score_of(gathered(own))
    matches[:, 0, :] = best
    matches[:, 1, :] = runner

    for o in range(m):
        arr[o, me] = own[o, me]
    for o in range(m):
        rest = arr.at[o, pl.ds(0, n - 1)]
        pltpu.make_async_copy(rest, rest, arr_recv.at[o]).wait()
    _, _, other_score = score_of(gathered(arr))
    asked_image = lists_in[:, 0, :][:, 0:1] // share
    for i in range(img_dev):
        scores[i] = jnp.sum(jnp.where(first == i, score, 0.0)) + jnp.sum(
            jnp.where(asked_image == i, other_score, 0.0)
        )

    def drain(ref, sem):
        pltpu.make_async_copy(ref, ref, sem).wait()

    drain(whole.at[pl.ds(0, 2)], ag_send)
    drain(whole.at[0], fw_send)
    drain(lists_out.at[pl.ds(0, n - 1)], list_send)
    drain(cands_out.at[pl.ds(0, n - 1)], cand_send)
    drain(own.at[pl.ds(0, m - 1)], own_send)
    drain(arr.at[:, pl.ds(0, n - 1)], arr_send)


def on_device(n, m, descriptors, cell_counts, pair_images, query_cells, cand_cells, cand_counts):
    img_dev, share, width = descriptors.shape
    rows, slots, qd = img_dev * share, cand_cells.shape[2], query_cells.shape[1] * width // DESC
    vmem = pl.BlockSpec(memory_space=pltpu.VMEM)
    dma = pltpu.SemaphoreType.DMA
    operands = (
        descriptors, cell_counts, pair_images.T, query_cells, cand_cells, cand_counts.T,
    )
    return pl.pallas_call(
        functools.partial(kernel, n, m),
        out_shape=(
            jax.ShapeDtypeStruct((n, 2, qd), f32),
            jax.ShapeDtypeStruct((img_dev,), f32),
        ),
        in_specs=[pl.BlockSpec(memory_space=pltpu.HBM)] * 6,
        out_specs=(vmem, pl.BlockSpec(memory_space=pltpu.SMEM)),
        scratch_shapes=[
            *(pltpu.VMEM(x.shape, x.dtype) for x in operands),
            dma((len(operands),)),
            pltpu.VMEM((m, rows, width), bf16),
            pltpu.VMEM((n, slots, rows), i32),
            pltpu.VMEM((n, slots, rows), i32),
            pltpu.VMEM((n, slots, width), bf16),
            pltpu.VMEM((n, slots, width), bf16),
            pltpu.VMEM((n, qd, 3 * DESC), bf16),
            pltpu.VMEM((n, 8, qd), f32),
            pltpu.VMEM((n, 2, qd), f32),
            pltpu.VMEM((m, n, 2, qd), f32),
            pltpu.VMEM((m, n, 2, qd), f32),
            dma, dma((2, img_dev)), dma, dma((img_dev,)),
            dma, dma((n,)), dma, dma((n,)),
            dma, dma((m,)), dma, dma((m,)),
        ],
        compiler_params=pltpu.CompilerParams(
            collective_id=0, has_side_effects=True
        ),
    )(*operands)


def solution(mesh):
    n, m = mesh.shape["img"], mesh.shape["rep"]
    in_specs = (
        P("img", "rep", None),
        P("img", "rep"),
        P("img", None),
        P("img", None),
        P("img", "rep", None),
        P("img", "rep"),
    )
    out_specs = (P("img", None, None), P("img"))
    return jax.shard_map(
        functools.partial(on_device, n, m),
        mesh=mesh, in_specs=in_specs, out_specs=out_specs, check_vma=False,
    )
```

```python
import functools

import jax
import jax.numpy as jnp
from jax import lax
from jax.experimental import pallas as pl
from jax.experimental.pallas import tpu as pltpu
from jax.sharding import PartitionSpec as P

DESC = 128
MESH = pl.DeviceIdType.MESH
distant = 1.0e9
far_entry = 32768.0
dead_mark = -1.0e9
f32, bf16, i32 = jnp.float32, jnp.bfloat16, jnp.int32


def partner(me, step, size):
    other, bit = 0, 1
    while bit < size:
        other = other + ((me // bit + step // bit) % 2) * bit
        bit *= 2
    return other


def repeat(first, last, body):
    if last - first <= 8:
        for t in range(first, last):
            body(t)
    else:
        lax.fori_loop(first, last, lambda t, c: (body(t), c)[1], 0)


def dot_t(a, b):
    return lax.dot_general(a, b, (((1,), (1,)), ((), ())), preferred_element_type=f32)


def split(square):
    high = square.astype(bf16)
    return high, (square - high.astype(f32)).astype(bf16)


def column(row, length):
    rows = lax.broadcasted_iota(i32, (length, length), 0)
    cols = lax.broadcasted_iota(i32, (length, length), 1)
    return jnp.sum(jnp.where(rows == cols, row, 0.0), axis=1, keepdims=True)


def merge(a, b):
    low = jnp.minimum(a[0], b[0])
    high = jnp.minimum(jnp.maximum(a[0], b[0]), jnp.minimum(a[1], b[1]))
    return low, high


def lowest_two(d):
    half = d.shape[0] // 2
    a, b = d[:half], d[half:]
    two = (jnp.minimum(a, b), jnp.maximum(a, b))
    while half > 1:
        half //= 2
        two = merge((two[0][:half], two[1][:half]), (two[0][half:], two[1][half:]))
    return two


def kernel(
    n, m,
    desc_hbm, counts_hbm, pairs_hbm, qcells_hbm, ccells_hbm, ccounts_hbm,
    matches, scores,
    desc, counts, pairs, qcells, ccells, ccounts, in_sem,
    whole, lists_out, lists_in, cands_out, cands_in, rhs, qnorm, part_out, own, arr,
    ag_send, ag_recv, fw_send, fw_recv, list_send, list_recv, cand_send, cand_recv,
    own_send, own_recv, arr_send, arr_recv,
):
    me, r = lax.axis_index("img"), lax.axis_index("rep")
    img_dev, share, width = desc.shape
    rows = img_dev * share
    kp = width // DESC
    slots = ccells.shape[2]
    qn = qcells.shape[1]
    mate, across = partner(r, 1, m), partner(r, 2, m)

    def remote(src, dst, send, recv, img, rep):
        return pltpu.make_async_remote_copy(
            src_ref=src, dst_ref=dst, send_sem=send, recv_sem=recv,
            device_id=(img, rep), device_id_type=MESH,
        )

    barrier = pltpu.get_barrier_semaphore()

    def greet(img, rep):
        pl.semaphore_signal(barrier, inc=1, device_id=(img, rep), device_id_type=MESH)

    repeat(1, n, lambda t: greet(partner(me, t, n), r))
    repeat(1, m, lambda t: greet(me, partner(r, t, m)))

    loads = [
        pltpu.make_async_copy(src, dst, in_sem.at[i])
        for i, (src, dst) in enumerate((
            (counts_hbm, counts), (desc_hbm, desc), (pairs_hbm, pairs),
            (ccells_hbm, ccells), (ccounts_hbm, ccounts), (qcells_hbm, qcells),
        ))
    ]
    for load in loads:
        load.start()
    for load in loads:
        load.wait()

    slot_of = lax.broadcasted_iota(i32, (share, width), 1) // DESC
    for i in range(img_dev):
        live = column(counts[i : i + 1, :].astype(f32), share)
        marked = jnp.where(slot_of.astype(f32) < live, desc[i].astype(f32), far_entry)
        whole[r, i * share : (i + 1) * share, :] = marked.astype(bf16)

    local = (pairs[...] % img_dev).astype(f32)
    first = column(local[0:1], n).astype(i32)
    second = column(local[1:2], n).astype(i32)
    live_cells = column(ccounts[...].astype(f32), n).astype(i32)
    wanted = second * share + ccells[:, 0, :] % share
    wanted = jnp.where(lax.broadcasted_iota(i32, (n, slots), 1) < live_cells, wanted, -1)
    wanted = jnp.concatenate([wanted, jnp.zeros((n, DESC - slots), i32)], axis=1)
    for j in range(n):
        lists_out[j] = wanted[j : j + 1]
    lists_in[me] = lists_out[me]

    pl.semaphore_wait(barrier, n + m - 2)

    def send_list(t):
        k = partner(me, t, n)
        remote(lists_out.at[k], lists_in.at[me], list_send, list_recv.at[me], k, r).start()

    repeat(1, n, send_list)

    def shard(owner, i):
        return whole.at[owner, pl.ds(i * share, share)]

    for i in range(img_dev):
        remote(shard(r, i), shard(r, i), ag_send, ag_recv.at[0, i], me, across).start()
    for i in range(img_dev):
        remote(shard(r, i), shard(r, i), ag_send, ag_recv.at[1, i], me, mate).start()

    group = n // 2
    for g in range(0, n, group):
        picks = []
        for t in range(g, g + group):
            k = partner(me, t, n)
            if t > 0:
                pltpu.make_async_copy(lists_out.at[k], lists_in.at[k], list_recv.at[k]).wait()
            picks.append(column(lists_in[k][:, :slots].astype(f32), slots))
        asked = jnp.concatenate(picks, axis=0).astype(i32)
        lanes = lax.broadcasted_iota(i32, (group * slots, rows), 1)
        chosen = (asked == lanes).astype(f32).astype(bf16)
        block = jnp.dot(chosen, whole[r], preferred_element_type=f32)
        block = jnp.where(asked < 0, far_entry, block).astype(bf16)
        for t in range(g, g + group):
            k = partner(me, t, n)
            part = block[(t - g) * slots : (t - g + 1) * slots]
            if t == 0:
                cands_in[me] = part
            else:
                cands_out[k] = part
        for t in range(max(g, 1), g + group):
            k = partner(me, t, n)
            remote(cands_out.at[k], cands_in.at[me], cand_send, cand_recv.at[me], k, r).start()

    for i in range(img_dev):
        pltpu.make_async_copy(shard(across, i), shard(across, i), ag_recv.at[0, i]).wait()
        remote(shard(across, i), shard(across, i), fw_send, fw_recv.at[i], me, mate).start()
    diagonal = partner(r, 3, m)
    for i in range(img_dev):
        pltpu.make_async_copy(shard(mate, i), shard(mate, i), ag_recv.at[1, i]).wait()
    for i in range(img_dev):
        pltpu.make_async_copy(shard(diagonal, i), shard(diagonal, i), fw_recv.at[i]).wait()

    cells = qcells[...]
    where = (cells // share) * rows + first * share + cells % share
    where = where.astype(f32)
    all_rows = m * rows
    picks = [
        jnp.broadcast_to(column(where[j : j + 1, :], qn), (qn, all_rows)) for j in range(n)
    ]
    asked = jnp.concatenate(picks, axis=0).astype(i32)
    chosen = (asked == lax.broadcasted_iota(i32, asked.shape, 1)).astype(f32).astype(bf16)
    found = jnp.dot(chosen, whole[...].reshape(all_rows, width), preferred_element_type=f32)
    found = found.astype(bf16)
    qd = qn * kp
    to = lax.broadcasted_iota(i32, (qd, qd), 0)
    at = lax.broadcasted_iota(i32, (qd, qd), 1)
    order = (at == (to % kp) * qn + to // kp).astype(f32).astype(bf16)
    ones = jnp.ones((qd, DESC), bf16)
    for j in range(n):
        mine = found[j * qn : (j + 1) * qn]
        stack = jnp.concatenate([mine[:, s * DESC : (s + 1) * DESC] for s in range(kp)], axis=0)
        query = jnp.dot(order, stack, preferred_element_type=f32)
        high, low = split(query * query)
        qnorm[j] = dot_t(jnp.ones((8, 2 * DESC), bf16), jnp.concatenate([high, low], axis=1))
        rhs[j] = jnp.concatenate([ones, ones, query.astype(bf16)], axis=1)

    def one_pair(t):
        j = partner(me, t, n)
        if not (isinstance(t, int) and t == 0):
            pltpu.make_async_copy(cands_out.at[j], cands_in.at[j], cand_recv.at[j]).wait()
        mine = cands_in[j]
        stack = jnp.concatenate([mine[:, s * DESC : (s + 1) * DESC] for s in range(kp)], axis=0)
        wide = stack.astype(f32)
        high, low = split(wide * wide)
        lhs = jnp.concatenate([high, low, (-2.0 * wide).astype(bf16)], axis=1)
        norm = qnorm[j][0:1]
        dist = jnp.minimum(dot_t(lhs, rhs[j]) + norm, distant)
        best, runner = lowest_two(dist)
        live = norm < distant
        two = jnp.concatenate(
            [jnp.where(live, best, dead_mark), jnp.where(live, runner, dead_mark)], axis=0
        )
        part_out[j] = two
        own[r, j] = two
        for d in range(1, m):
            to_rep = partner(r, d, m)
            remote(part_out.at[j], own.at[r, j], own_send, own_recv.at[r], me, to_rep).start()
        if not (isinstance(t, int) and t == 0):
            for d in range(m):
                to_rep = partner(r, d, m)
                remote(part_out.at[j], arr.at[r, me], arr_send, arr_recv.at[r], j, to_rep).start()

    one_pair(0)
    repeat(1, n, one_pair)

    for d in range(1, m):
        o = partner(r, d, m)
        pltpu.make_async_copy(own.at[o], own.at[o], own_recv.at[o]).wait()

    def gathered(buf):
        two = (buf[0, :, 0, :], buf[0, :, 1, :])
        for o in range(1, m):
            two = merge(two, (buf[o, :, 0, :], buf[o, :, 1, :]))
        return two

    def score_of(two):
        live = two[0] > 0.5 * dead_mark
        best, runner = jnp.where(live, two[0], 0.0), jnp.where(live, two[1], 0.0)
        margin = jnp.where(live, (runner - best) / (runner + 1.0), 0.0)
        total = jnp.sum(margin, axis=1, keepdims=True)
        return best, runner, total / jnp.sum(live.astype(f32), axis=1, keepdims=True)

    best, runner, score = score_of(gathered(own))
    matches[:, 0, :] = best
    matches[:, 1, :] = runner

    for o in range(m):
        arr[o, me] = own[o, me]
    for o in range(m):
        rest = arr.at[o, pl.ds(0, n - 1)]
        pltpu.make_async_copy(rest, rest, arr_recv.at[o]).wait()
    _, _, other_score = score_of(gathered(arr))
    asked_image = lists_in[:, 0, :][:, 0:1] // share
    for i in range(img_dev):
        scores[i] = jnp.sum(jnp.where(first == i, score, 0.0)) + jnp.sum(
            jnp.where(asked_image == i, other_score, 0.0)
        )

    def drain(ref, sem):
        pltpu.make_async_copy(ref, ref, sem).wait()

    drain(whole.at[pl.ds(0, 2)], ag_send)
    drain(whole.at[0], fw_send)
    drain(lists_out.at[pl.ds(0, n - 1)], list_send)
    drain(cands_out.at[pl.ds(0, n - 1)], cand_send)
    drain(own.at[pl.ds(0, m - 1)], own_send)
    drain(arr.at[:, pl.ds(0, n - 1)], arr_send)


def on_device(n, m, descriptors, cell_counts, pair_images, query_cells, cand_cells, cand_counts):
    img_dev, share, width = descriptors.shape
    rows, slots, qd = img_dev * share, cand_cells.shape[2], query_cells.shape[1] * width // DESC
    vmem = pl.BlockSpec(memory_space=pltpu.VMEM)
    dma = pltpu.SemaphoreType.DMA
    operands = (
        descriptors, cell_counts, pair_images.T, query_cells, cand_cells, cand_counts.T,
    )
    return pl.pallas_call(
        functools.partial(kernel, n, m),
        out_shape=(
            jax.ShapeDtypeStruct((n, 2, qd), f32),
            jax.ShapeDtypeStruct((img_dev,), f32),
        ),
        in_specs=[pl.BlockSpec(memory_space=pltpu.HBM)] * 6,
        out_specs=(vmem, pl.BlockSpec(memory_space=pltpu.SMEM)),
        scratch_shapes=[
            *(pltpu.VMEM(x.shape, x.dtype) for x in operands),
            dma((len(operands),)),
            pltpu.VMEM((m, rows, width), bf16),
            pltpu.VMEM((n, 1, DESC), i32),
            pltpu.VMEM((n, 1, DESC), i32),
            pltpu.VMEM((n, slots, width), bf16),
            pltpu.VMEM((n, slots, width), bf16),
            pltpu.VMEM((n, qd, 3 * DESC), bf16),
            pltpu.VMEM((n, 8, qd), f32),
            pltpu.VMEM((n, 2, qd), f32),
            pltpu.VMEM((m, n, 2, qd), f32),
            pltpu.VMEM((m, n, 2, qd), f32),
            dma, dma((2, img_dev)), dma, dma((img_dev,)),
            dma, dma((n,)), dma, dma((n,)),
            dma, dma((m,)), dma, dma((m,)),
        ],
        compiler_params=pltpu.CompilerParams(
            collective_id=0, has_side_effects=True
        ),
    )(*operands)


def solution(mesh):
    n, m = mesh.shape["img"], mesh.shape["rep"]
    in_specs = (
        P("img", "rep", None),
        P("img", "rep"),
        P("img", None),
        P("img", None),
        P("img", "rep", None),
        P("img", "rep"),
    )
    out_specs = (P("img", None, None), P("img"))
    return jax.shard_map(
        functools.partial(on_device, n, m),
        mesh=mesh, in_specs=in_specs, out_specs=out_specs, check_vma=False,
    )
```

```python
import functools

import jax
import jax.numpy as jnp
from jax import lax
from jax.experimental import pallas as pl
from jax.experimental.pallas import tpu as pltpu
from jax.sharding import PartitionSpec as P

DESC = 128
MESH = pl.DeviceIdType.MESH
distant = 1.0e9
far_entry = 32768.0
dead_mark = -1.0e9
f32, bf16, i32 = jnp.float32, jnp.bfloat16, jnp.int32


def partner(me, step, size):
    other, bit = 0, 1
    while bit < size:
        other = other + ((me // bit + step // bit) % 2) * bit
        bit *= 2
    return other


def repeat(first, last, body):
    if last - first <= 8:
        for t in range(first, last):
            body(t)
    else:
        lax.fori_loop(first, last, lambda t, c: (body(t), c)[1], 0)


def dot_t(a, b):
    return lax.dot_general(a, b, (((1,), (1,)), ((), ())), preferred_element_type=f32)


def split(square):
    high = square.astype(bf16)
    return high, (square - high.astype(f32)).astype(bf16)


def column(row, length):
    rows = lax.broadcasted_iota(i32, (length, length), 0)
    cols = lax.broadcasted_iota(i32, (length, length), 1)
    return jnp.sum(jnp.where(rows == cols, row, 0.0), axis=1, keepdims=True)


def merge(a, b):
    low = jnp.minimum(a[0], b[0])
    high = jnp.minimum(jnp.maximum(a[0], b[0]), jnp.minimum(a[1], b[1]))
    return low, high


def lowest_two(d):
    half = d.shape[0] // 2
    a, b = d[:half], d[half:]
    two = (jnp.minimum(a, b), jnp.maximum(a, b))
    while half > 1:
        half //= 2
        two = merge((two[0][:half], two[1][:half]), (two[0][half:], two[1][half:]))
    return two


def kernel(
    n, m,
    desc_hbm, counts_hbm, pairs_hbm, qcells_hbm, ccells_hbm, ccounts_hbm,
    own, arr, lists_hbm,
    desc, counts, pairs, qcells, ccells, ccounts, in_sem,
    whole, lists_out, lists_in, cands_out, cands_in, rhs, qnorm, part_out, out_sem,
    ag_send, ag_recv, fw_send, fw_recv, list_send, list_recv, cand_send, cand_recv,
    own_send, own_recv, arr_send, arr_recv,
):
    me, r = lax.axis_index("img"), lax.axis_index("rep")
    img_dev, share, width = desc.shape
    rows = img_dev * share
    kp = width // DESC
    slots = ccells.shape[2]
    qn = qcells.shape[1]
    mate, across = partner(r, 1, m), partner(r, 2, m)

    def remote(src, dst, send, recv, img, rep):
        return pltpu.make_async_remote_copy(
            src_ref=src, dst_ref=dst, send_sem=send, recv_sem=recv,
            device_id=(img, rep), device_id_type=MESH,
        )

    barrier = pltpu.get_barrier_semaphore()

    def greet(img, rep):
        pl.semaphore_signal(barrier, inc=1, device_id=(img, rep), device_id_type=MESH)

    repeat(1, n, lambda t: greet(partner(me, t, n), r))
    repeat(1, m, lambda t: greet(me, partner(r, t, m)))

    loads = [
        pltpu.make_async_copy(src, dst, in_sem.at[i])
        for i, (src, dst) in enumerate((
            (counts_hbm, counts), (desc_hbm, desc), (pairs_hbm, pairs),
            (ccells_hbm, ccells), (ccounts_hbm, ccounts), (qcells_hbm, qcells),
        ))
    ]
    for load in loads:
        load.start()
    for load in loads:
        load.wait()

    slot_of = lax.broadcasted_iota(i32, (share, width), 1) // DESC
    for i in range(img_dev):
        live = column(counts[i : i + 1, :].astype(f32), share)
        marked = jnp.where(slot_of.astype(f32) < live, desc[i].astype(f32), far_entry)
        whole[r, i * share : (i + 1) * share, :] = marked.astype(bf16)

    local = (pairs[...] % img_dev).astype(f32)
    first = column(local[0:1], n).astype(i32)
    second = column(local[1:2], n).astype(i32)
    live_cells = column(ccounts[...].astype(f32), n).astype(i32)
    wanted = second * share + ccells[:, 0, :] % share
    wanted = jnp.where(lax.broadcasted_iota(i32, (n, slots), 1) < live_cells, wanted, -1)
    wanted = jnp.concatenate([wanted, jnp.zeros((n, DESC - slots), i32)], axis=1)
    for j in range(n):
        lists_out[j] = wanted[j : j + 1]
    lists_in[me] = lists_out[me]

    pl.semaphore_wait(barrier, n + m - 2)

    def send_list(t):
        k = partner(me, t, n)
        remote(lists_out.at[k], lists_in.at[me], list_send, list_recv.at[me], k, r).start()

    repeat(1, n, send_list)

    def shard(owner, i):
        return whole.at[owner, pl.ds(i * share, share)]

    for i in range(img_dev):
        remote(shard(r, i), shard(r, i), ag_send, ag_recv.at[0, i], me, across).start()
    for i in range(img_dev):
        remote(shard(r, i), shard(r, i), ag_send, ag_recv.at[1, i], me, mate).start()

    group = n // 2
    for g in range(0, n, group):
        picks = []
        for t in range(g, g + group):
            k = partner(me, t, n)
            if t > 0:
                pltpu.make_async_copy(lists_out.at[k], lists_in.at[k], list_recv.at[k]).wait()
            picks.append(column(lists_in[k][:, :slots].astype(f32), slots))
        asked = jnp.concatenate(picks, axis=0).astype(i32)
        lanes = lax.broadcasted_iota(i32, (group * slots, rows), 1)
        chosen = (asked == lanes).astype(f32).astype(bf16)
        block = jnp.dot(chosen, whole[r], preferred_element_type=f32)
        block = jnp.where(asked < 0, far_entry, block).astype(bf16)
        for t in range(g, g + group):
            k = partner(me, t, n)
            part = block[(t - g) * slots : (t - g + 1) * slots]
            if t == 0:
                cands_in[me] = part
            else:
                cands_out[k] = part
        for t in range(max(g, 1), g + group):
            k = partner(me, t, n)
            remote(cands_out.at[k], cands_in.at[me], cand_send, cand_recv.at[me], k, r).start()

    listed = pltpu.make_async_copy(lists_in, lists_hbm, out_sem.at[0])
    listed.start()

    for i in range(img_dev):
        pltpu.make_async_copy(shard(across, i), shard(across, i), ag_recv.at[0, i]).wait()
        remote(shard(across, i), shard(across, i), fw_send, fw_recv.at[i], me, mate).start()
    diagonal = partner(r, 3, m)
    for i in range(img_dev):
        pltpu.make_async_copy(shard(mate, i), shard(mate, i), ag_recv.at[1, i]).wait()
    for i in range(img_dev):
        pltpu.make_async_copy(shard(diagonal, i), shard(diagonal, i), fw_recv.at[i]).wait()

    cells = qcells[...]
    where = (cells // share) * rows + first * share + cells % share
    where = where.astype(f32)
    all_rows = m * rows
    picks = [
        jnp.broadcast_to(column(where[j : j + 1, :], qn), (qn, all_rows)) for j in range(n)
    ]
    asked = jnp.concatenate(picks, axis=0).astype(i32)
    chosen = (asked == lax.broadcasted_iota(i32, asked.shape, 1)).astype(f32).astype(bf16)
    found = jnp.dot(chosen, whole[...].reshape(all_rows, width), preferred_element_type=f32)
    found = found.astype(bf16)
    qd = qn * kp
    to = lax.broadcasted_iota(i32, (qd, qd), 0)
    at = lax.broadcasted_iota(i32, (qd, qd), 1)
    order = (at == (to % kp) * qn + to // kp).astype(f32).astype(bf16)
    ones = jnp.ones((qd, DESC), bf16)
    for j in range(n):
        mine = found[j * qn : (j + 1) * qn]
        stack = jnp.concatenate([mine[:, s * DESC : (s + 1) * DESC] for s in range(kp)], axis=0)
        query = jnp.dot(order, stack, preferred_element_type=f32)
        high, low = split(query * query)
        qnorm[j] = dot_t(jnp.ones((8, 2 * DESC), bf16), jnp.concatenate([high, low], axis=1))
        rhs[j] = jnp.concatenate([ones, ones, query.astype(bf16)], axis=1)

    def one_pair(t):
        j = partner(me, t, n)
        if not (isinstance(t, int) and t == 0):
            pltpu.make_async_copy(cands_out.at[j], cands_in.at[j], cand_recv.at[j]).wait()
        mine = cands_in[j]
        stack = jnp.concatenate([mine[:, s * DESC : (s + 1) * DESC] for s in range(kp)], axis=0)
        wide = stack.astype(f32)
        high, low = split(wide * wide)
        lhs = jnp.concatenate([high, low, (-2.0 * wide).astype(bf16)], axis=1)
        norm = qnorm[j][0:1]
        dist = jnp.minimum(dot_t(lhs, rhs[j]) + norm, distant)
        best, runner = lowest_two(dist)
        live = norm < distant
        two = jnp.concatenate(
            [jnp.where(live, best, dead_mark), jnp.where(live, runner, dead_mark)], axis=0
        )
        part_out[j] = two
        for d in range(1, m):
            to_rep = partner(r, d, m)
            remote(part_out.at[j], own.at[r, j], own_send, own_recv.at[r], me, to_rep).start()
        if not (isinstance(t, int) and t == 0):
            for d in range(m):
                to_rep = partner(r, d, m)
                remote(part_out.at[j], arr.at[r, me], arr_send, arr_recv.at[r], j, to_rep).start()

    one_pair(0)
    repeat(1, n, one_pair)

    mine = pltpu.make_async_copy(part_out, own.at[r], out_sem.at[1])
    mine.start()
    listed.wait()
    mine.wait()
    for d in range(1, m):
        o = partner(r, d, m)
        pltpu.make_async_copy(own.at[o], own.at[o], own_recv.at[o]).wait()
    for o in range(m):
        rest = arr.at[o, pl.ds(0, n - 1)]
        pltpu.make_async_copy(rest, rest, arr_recv.at[o]).wait()

    def drain(ref, sem):
        pltpu.make_async_copy(ref, ref, sem).wait()

    drain(whole.at[pl.ds(0, 2)], ag_send)
    drain(whole.at[0], fw_send)
    drain(lists_out.at[pl.ds(0, n - 1)], list_send)
    drain(cands_out.at[pl.ds(0, n - 1)], cand_send)
    drain(own.at[pl.ds(0, m - 1)], own_send)
    drain(arr.at[:, pl.ds(0, n - 1)], arr_send)


def finish(n, m, img_dev, share, own, arr, lists, pairs, matches, scores):
    me = lax.axis_index("img")

    def gathered(buf):
        two = (buf[0, :, 0, :], buf[0, :, 1, :])
        for o in range(1, m):
            two = merge(two, (buf[o, :, 0, :], buf[o, :, 1, :]))
        return two

    def score_of(two):
        live = two[0] > 0.5 * dead_mark
        best, runner = jnp.where(live, two[0], 0.0), jnp.where(live, two[1], 0.0)
        margin = jnp.where(live, (runner - best) / (runner + 1.0), 0.0)
        total = jnp.sum(margin, axis=1, keepdims=True)
        return best, runner, total / jnp.sum(live.astype(f32), axis=1, keepdims=True)

    best, runner, score = score_of(gathered(own))
    matches[:, 0, :] = best
    matches[:, 1, :] = runner
    _, _, other_score = score_of(gathered(arr))
    other_score = jnp.where(lax.broadcasted_iota(i32, (n, 1), 0) == me, score, other_score)
    asked_image = lists[:, 0, :][:, 0:1] // share
    first = column((pairs[0:1] % img_dev).astype(f32), n).astype(i32)
    for i in range(img_dev):
        scores[i] = jnp.sum(jnp.where(first == i, score, 0.0)) + jnp.sum(
            jnp.where(asked_image == i, other_score, 0.0)
        )


def on_device(n, m, descriptors, cell_counts, pair_images, query_cells, cand_cells, cand_counts):
    img_dev, share, width = descriptors.shape
    rows, slots, qd = img_dev * share, cand_cells.shape[2], query_cells.shape[1] * width // DESC
    vmem = pl.BlockSpec(memory_space=pltpu.VMEM)
    dma = pltpu.SemaphoreType.DMA
    operands = (
        descriptors, cell_counts, pair_images.T, query_cells, cand_cells, cand_counts.T,
    )
    hbm = pl.BlockSpec(memory_space=pltpu.HBM)
    partial = jax.ShapeDtypeStruct((m, n, 2, qd), f32)
    own, arr, lists = pl.pallas_call(
        functools.partial(kernel, n, m),
        out_shape=(partial, partial, jax.ShapeDtypeStruct((n, 1, DESC), i32)),
        in_specs=[hbm] * 6,
        out_specs=(hbm,) * 3,
        scratch_shapes=[
            *(pltpu.VMEM(x.shape, x.dtype) for x in operands),
            dma((len(operands),)),
            pltpu.VMEM((m, rows, width), bf16),
            pltpu.VMEM((n, 1, DESC), i32),
            pltpu.VMEM((n, 1, DESC), i32),
            pltpu.VMEM((n, slots, width), bf16),
            pltpu.VMEM((n, slots, width), bf16),
            pltpu.VMEM((n, qd, 3 * DESC), bf16),
            pltpu.VMEM((n, 8, qd), f32),
            pltpu.VMEM((n, 2, qd), f32),
            dma((2,)),
            dma, dma((2, img_dev)), dma, dma((img_dev,)),
            dma, dma((n,)), dma, dma((n,)),
            dma, dma((m,)), dma, dma((m,)),
        ],
        compiler_params=pltpu.CompilerParams(
            collective_id=0, has_side_effects=True
        ),
    )(*operands)
    return pl.pallas_call(
        functools.partial(finish, n, m, img_dev, share),
        out_shape=(
            jax.ShapeDtypeStruct((n, 2, qd), f32),
            jax.ShapeDtypeStruct((img_dev,), f32),
        ),
        in_specs=[vmem] * 4,
        out_specs=(vmem, pl.BlockSpec(memory_space=pltpu.SMEM)),
    )(own, arr, lists, pair_images.T)


def solution(mesh):
    n, m = mesh.shape["img"], mesh.shape["rep"]
    in_specs = (
        P("img", "rep", None),
        P("img", "rep"),
        P("img", None),
        P("img", None),
        P("img", "rep", None),
        P("img", "rep"),
    )
    out_specs = (P("img", None, None), P("img"))
    return jax.shard_map(
        functools.partial(on_device, n, m),
        mesh=mesh, in_specs=in_specs, out_specs=out_specs, check_vma=False,
    )
```

```python
import functools

import jax
import jax.numpy as jnp
from jax import lax
from jax.experimental import pallas as pl
from jax.experimental.pallas import tpu as pltpu
from jax.sharding import PartitionSpec as P

DESC = 128
MESH = pl.DeviceIdType.MESH
distant = 1.0e9
far_entry = 32768.0
dead_mark = -1.0e9
f32, bf16, i32 = jnp.float32, jnp.bfloat16, jnp.int32


def partner(me, step, size):
    other, bit = 0, 1
    while bit < size:
        other = other + ((me // bit + step // bit) % 2) * bit
        bit *= 2
    return other


def repeat(first, last, body):
    if last - first <= 8:
        for t in range(first, last):
            body(t)
    else:
        lax.fori_loop(first, last, lambda t, c: (body(t), c)[1], 0)


def dot_t(a, b):
    return lax.dot_general(a, b, (((1,), (1,)), ((), ())), preferred_element_type=f32)


def split(square):
    high = square.astype(bf16)
    return high, (square - high.astype(f32)).astype(bf16)


def column(row, length):
    rows = lax.broadcasted_iota(i32, (length, length), 0)
    cols = lax.broadcasted_iota(i32, (length, length), 1)
    return jnp.sum(jnp.where(rows == cols, row, 0.0), axis=1, keepdims=True)


def merge(a, b):
    low = jnp.minimum(a[0], b[0])
    high = jnp.minimum(jnp.maximum(a[0], b[0]), jnp.minimum(a[1], b[1]))
    return low, high


def lowest_two(d):
    half = d.shape[0] // 2
    a, b = d[:half], d[half:]
    two = (jnp.minimum(a, b), jnp.maximum(a, b))
    while half > 1:
        half //= 2
        two = merge((two[0][:half], two[1][:half]), (two[0][half:], two[1][half:]))
    return two


def kernel(
    n, m,
    desc_hbm, counts_hbm, pairs_hbm, qcells_hbm, ccells_hbm, ccounts_hbm,
    own, arr, lists_hbm,
    desc, counts, pairs, qcells, ccells, ccounts, in_sem,
    whole, lists_out, lists_in, cands_out, cands_in, rhs, qnorm, part_out, out_sem,
    ag_send, ag_recv, fw_send, fw_recv, list_send, list_recv, cand_send, cand_recv,
    own_send, own_recv, arr_send, arr_recv,
):
    me, r = lax.axis_index("img"), lax.axis_index("rep")
    img_dev, share, width = desc.shape
    rows = img_dev * share
    kp = width // DESC
    slots = ccells.shape[2]
    qn = qcells.shape[1]
    mate, across = partner(r, 1, m), partner(r, 2, m)

    def remote(src, dst, send, recv, img, rep):
        return pltpu.make_async_remote_copy(
            src_ref=src, dst_ref=dst, send_sem=send, recv_sem=recv,
            device_id=(img, rep), device_id_type=MESH,
        )

    barrier = pltpu.get_barrier_semaphore()

    def greet(img, rep):
        pl.semaphore_signal(barrier, inc=1, device_id=(img, rep), device_id_type=MESH)

    repeat(1, n, lambda t: greet(partner(me, t, n), r))
    repeat(1, m, lambda t: greet(me, partner(r, t, m)))

    loads = [
        pltpu.make_async_copy(src, dst, in_sem.at[i])
        for i, (src, dst) in enumerate((
            (counts_hbm, counts), (desc_hbm, desc), (pairs_hbm, pairs),
            (ccells_hbm, ccells), (ccounts_hbm, ccounts), (qcells_hbm, qcells),
        ))
    ]
    for load in loads:
        load.start()
    for load in loads:
        load.wait()

    slot_of = lax.broadcasted_iota(i32, (share, width), 1) // DESC
    for i in range(img_dev):
        live = column(counts[i : i + 1, :].astype(f32), share)
        marked = jnp.where(slot_of.astype(f32) < live, desc[i].astype(f32), far_entry)
        whole[r, i * share : (i + 1) * share, :] = marked.astype(bf16)

    local = (pairs[...] % img_dev).astype(f32)
    first = column(local[0:1], n).astype(i32)
    second = column(local[1:2], n).astype(i32)
    live_cells = column(ccounts[...].astype(f32), n).astype(i32)
    wanted = second * share + ccells[:, 0, :] % share
    wanted = jnp.where(lax.broadcasted_iota(i32, (n, slots), 1) < live_cells, wanted, -1)
    wanted = jnp.concatenate([wanted, jnp.zeros((n, DESC - slots), i32)], axis=1)
    for j in range(n):
        lists_out[j] = wanted[j : j + 1]
    lists_in[me] = lists_out[me]

    pl.semaphore_wait(barrier, n + m - 2)

    def send_list(t):
        k = partner(me, t, n)
        remote(lists_out.at[k], lists_in.at[me], list_send, list_recv.at[me], k, r).start()

    repeat(1, n, send_list)

    def shard(owner, i):
        return whole.at[owner, pl.ds(i * share, share)]

    for i in range(img_dev):
        remote(shard(r, i), shard(r, i), ag_send, ag_recv.at[0, i], me, across).start()
    for i in range(img_dev):
        remote(shard(r, i), shard(r, i), ag_send, ag_recv.at[1, i], me, mate).start()

    group = n // 2
    for g in (group, 0):
        picks = []
        for t in range(g, g + group):
            k = partner(me, t, n)
            if t > 0:
                pltpu.make_async_copy(lists_out.at[k], lists_in.at[k], list_recv.at[k]).wait()
            picks.append(column(lists_in[k][:, :slots].astype(f32), slots))
        asked = jnp.concatenate(picks, axis=0).astype(i32)
        lanes = lax.broadcasted_iota(i32, (group * slots, rows), 1)
        chosen = (asked == lanes).astype(f32).astype(bf16)
        block = jnp.dot(chosen, whole[r], preferred_element_type=f32)
        block = jnp.where(asked < 0, far_entry, block).astype(bf16)
        for t in range(g, g + group):
            k = partner(me, t, n)
            part = block[(t - g) * slots : (t - g + 1) * slots]
            if t == 0:
                cands_in[me] = part
            else:
                cands_out[k] = part
        for t in range(max(g, 1), g + group):
            k = partner(me, t, n)
            remote(cands_out.at[k], cands_in.at[me], cand_send, cand_recv.at[me], k, r).start()

    listed = pltpu.make_async_copy(lists_in, lists_hbm, out_sem.at[0])
    listed.start()

    for i in range(img_dev):
        pltpu.make_async_copy(shard(across, i), shard(across, i), ag_recv.at[0, i]).wait()
        remote(shard(across, i), shard(across, i), fw_send, fw_recv.at[i], me, mate).start()
    diagonal = partner(r, 3, m)
    for i in range(img_dev):
        pltpu.make_async_copy(shard(mate, i), shard(mate, i), ag_recv.at[1, i]).wait()
    for i in range(img_dev):
        pltpu.make_async_copy(shard(diagonal, i), shard(diagonal, i), fw_recv.at[i]).wait()

    cells = qcells[...]
    where = (cells // share) * rows + first * share + cells % share
    where = where.astype(f32)
    all_rows = m * rows
    picks = [
        jnp.broadcast_to(column(where[j : j + 1, :], qn), (qn, all_rows)) for j in range(n)
    ]
    asked = jnp.concatenate(picks, axis=0).astype(i32)
    chosen = (asked == lax.broadcasted_iota(i32, asked.shape, 1)).astype(f32).astype(bf16)
    found = jnp.dot(chosen, whole[...].reshape(all_rows, width), preferred_element_type=f32)
    found = found.astype(bf16)
    qd = qn * kp
    to = lax.broadcasted_iota(i32, (qd, qd), 0)
    at = lax.broadcasted_iota(i32, (qd, qd), 1)
    order = (at == (to % kp) * qn + to // kp).astype(f32).astype(bf16)
    ones = jnp.ones((qd, DESC), bf16)
    for j in range(n):
        mine = found[j * qn : (j + 1) * qn]
        stack = jnp.concatenate([mine[:, s * DESC : (s + 1) * DESC] for s in range(kp)], axis=0)
        query = jnp.dot(order, stack, preferred_element_type=f32)
        high, low = split(query * query)
        qnorm[j] = dot_t(jnp.ones((8, 2 * DESC), bf16), jnp.concatenate([high, low], axis=1))
        rhs[j] = jnp.concatenate([ones, ones, query.astype(bf16)], axis=1)

    def one_pair(t):
        j = partner(me, t, n)
        if not (isinstance(t, int) and t == 0):
            pltpu.make_async_copy(cands_out.at[j], cands_in.at[j], cand_recv.at[j]).wait()
        mine = cands_in[j]
        stack = jnp.concatenate([mine[:, s * DESC : (s + 1) * DESC] for s in range(kp)], axis=0)
        wide = stack.astype(f32)
        high, low = split(wide * wide)
        lhs = jnp.concatenate([high, low, (-2.0 * wide).astype(bf16)], axis=1)
        norm = qnorm[j][0:1]
        dist = jnp.minimum(dot_t(lhs, rhs[j]) + norm, distant)
        best, runner = lowest_two(dist)
        live = norm < distant
        two = jnp.concatenate(
            [jnp.where(live, best, dead_mark), jnp.where(live, runner, dead_mark)], axis=0
        )
        part_out[j] = two
        if not (isinstance(t, int) and t == 0):
            for d in range(m):
                to_rep = partner(r, d, m)
                remote(part_out.at[j], arr.at[r, me], arr_send, arr_recv.at[r], j, to_rep).start()
        for d in range(1, m):
            to_rep = partner(r, d, m)
            remote(part_out.at[j], own.at[r, j], own_send, own_recv.at[r], me, to_rep).start()

    one_pair(0)
    repeat(1, n, one_pair)

    mine = pltpu.make_async_copy(part_out, own.at[r], out_sem.at[1])
    mine.start()
    listed.wait()
    mine.wait()
    for d in range(1, m):
        o = partner(r, d, m)
        pltpu.make_async_copy(own.at[o], own.at[o], own_recv.at[o]).wait()
    for o in range(m):
        rest = arr.at[o, pl.ds(0, n - 1)]
        pltpu.make_async_copy(rest, rest, arr_recv.at[o]).wait()

    def drain(ref, sem):
        pltpu.make_async_copy(ref, ref, sem).wait()

    drain(whole.at[pl.ds(0, 2)], ag_send)
    drain(whole.at[0], fw_send)
    drain(lists_out.at[pl.ds(0, n - 1)], list_send)
    drain(cands_out.at[pl.ds(0, n - 1)], cand_send)
    drain(own.at[pl.ds(0, m - 1)], own_send)
    drain(arr.at[:, pl.ds(0, n - 1)], arr_send)


def finish(n, m, img_dev, share, own, arr, lists, pairs, matches, scores):
    me = lax.axis_index("img")

    def gathered(buf):
        two = (buf[0, :, 0, :], buf[0, :, 1, :])
        for o in range(1, m):
            two = merge(two, (buf[o, :, 0, :], buf[o, :, 1, :]))
        return two

    def score_of(two):
        live = two[0] > 0.5 * dead_mark
        best, runner = jnp.where(live, two[0], 0.0), jnp.where(live, two[1], 0.0)
        margin = jnp.where(live, (runner - best) / (runner + 1.0), 0.0)
        total = jnp.sum(margin, axis=1, keepdims=True)
        return best, runner, total / jnp.sum(live.astype(f32), axis=1, keepdims=True)

    best, runner, score = score_of(gathered(own))
    matches[:, 0, :] = best
    matches[:, 1, :] = runner
    _, _, other_score = score_of(gathered(arr))
    other_score = jnp.where(lax.broadcasted_iota(i32, (n, 1), 0) == me, score, other_score)
    asked_image = lists[:, 0, :][:, 0:1] // share
    first = column((pairs[0:1] % img_dev).astype(f32), n).astype(i32)
    for i in range(img_dev):
        scores[i] = jnp.sum(jnp.where(first == i, score, 0.0)) + jnp.sum(
            jnp.where(asked_image == i, other_score, 0.0)
        )


def on_device(n, m, descriptors, cell_counts, pair_images, query_cells, cand_cells, cand_counts):
    img_dev, share, width = descriptors.shape
    rows, slots, qd = img_dev * share, cand_cells.shape[2], query_cells.shape[1] * width // DESC
    vmem = pl.BlockSpec(memory_space=pltpu.VMEM)
    dma = pltpu.SemaphoreType.DMA
    operands = (
        descriptors, cell_counts, pair_images.T, query_cells, cand_cells, cand_counts.T,
    )
    hbm = pl.BlockSpec(memory_space=pltpu.HBM)
    partial = jax.ShapeDtypeStruct((m, n, 2, qd), f32)
    own, arr, lists = pl.pallas_call(
        functools.partial(kernel, n, m),
        out_shape=(partial, partial, jax.ShapeDtypeStruct((n, 1, DESC), i32)),
        in_specs=[hbm] * 6,
        out_specs=(hbm,) * 3,
        scratch_shapes=[
            *(pltpu.VMEM(x.shape, x.dtype) for x in operands),
            dma((len(operands),)),
            pltpu.VMEM((m, rows, width), bf16),
            pltpu.VMEM((n, 1, DESC), i32),
            pltpu.VMEM((n, 1, DESC), i32),
            pltpu.VMEM((n, slots, width), bf16),
            pltpu.VMEM((n, slots, width), bf16),
            pltpu.VMEM((n, qd, 3 * DESC), bf16),
            pltpu.VMEM((n, 8, qd), f32),
            pltpu.VMEM((n, 2, qd), f32),
            dma((2,)),
            dma, dma((2, img_dev)), dma, dma((img_dev,)),
            dma, dma((n,)), dma, dma((n,)),
            dma, dma((m,)), dma, dma((m,)),
        ],
        compiler_params=pltpu.CompilerParams(
            collective_id=0, has_side_effects=True
        ),
    )(*operands)
    return pl.pallas_call(
        functools.partial(finish, n, m, img_dev, share),
        out_shape=(
            jax.ShapeDtypeStruct((n, 2, qd), f32),
            jax.ShapeDtypeStruct((img_dev,), f32),
        ),
        in_specs=[vmem] * 4,
        out_specs=(vmem, pl.BlockSpec(memory_space=pltpu.SMEM)),
    )(own, arr, lists, pair_images.T)


def solution(mesh):
    n, m = mesh.shape["img"], mesh.shape["rep"]
    in_specs = (
        P("img", "rep", None),
        P("img", "rep"),
        P("img", None),
        P("img", None),
        P("img", "rep", None),
        P("img", "rep"),
    )
    out_specs = (P("img", None, None), P("img"))
    return jax.shard_map(
        functools.partial(on_device, n, m),
        mesh=mesh, in_specs=in_specs, out_specs=out_specs, check_vma=False,
    )
```
